32 devices in a mesh: ctx: 2 (over y), ch: 16 (over z, x, core).
Axes of the slice: x: 2, y: 2, z: 4, core: 2. Of those that a mesh axis runs over, the one named last changes fastest.
Arguments:
- projections: bfloat16 [4, 1024, 3, 4096], P(None, ('ctx', 'ch')), may hold values from -6 to 6
- impulse: float32 [1024, 4096], P('ctx', 'ch'), may hold values from -4 to 4, as said below
- skip_gain: float32 [4096], P('ch'), may hold values from 0.3 to 1.5
Outputs:
- gated: bfloat16 [4, 1024, 4096], P(None, ('ctx', 'ch'))
The draws below stay inside these ranges and needn't reach their ends.
Inputs may be any that keep to these rules, and one draw needn't show every extreme that they name: impulse holds a filter of each channel over lags.
All inputs are finite; a program needn't handle non-finite values.
Results may differ from the reference program's by a relative error of at most 0.0056.
Values may be sent and summed in bfloat16 or wider, within the bound.
A program may use at most 128 MiB of HBM per device.

```python
import math
import jax
import jax.numpy as jnp
from jax import lax

D = 4096
SPAN = 512
SEQS = 4
LEN = 1024


def draw_impulse(key, part):
    noise_key = jax.random.fold_in(key, 11)
    reach_key = jax.random.fold_in(key, 12)
    lag_rows = jnp.arange(LEN, dtype=jnp.float32)[:, None]
    decay_length = LEN * jnp.exp(jax.random.uniform(reach_key, (1, D), jnp.float32, math.log(0.02), math.log(10.0)))
    rough_part = jax.random.truncated_normal(noise_key, -4.0, 4.0, (LEN, D), jnp.float32)
    amplitude = jnp.sqrt(2.0 / decay_length / (1.0 - jnp.exp(-2.0 * LEN / decay_length)))
    return (rough_part * amplitude * jnp.exp(-lag_rows / decay_length)).astype(jnp.float32)


def level_of(stream_key, dims, pieces, smallest, top_value):
    loudness, own = 1.0, jax.random.fold_in(stream_key, 6)
    for dim, shards_of in pieces:
        draws = jnp.exp(jax.random.uniform(jax.random.fold_in(own, dim), (shards_of,), jnp.float32, smallest / len(pieces), top_value / len(pieces)))
        loudness = loudness * jnp.repeat(draws, dims[dim] // shards_of).reshape([-1 if axis == dim else 1 for axis in range(len(dims))])
    return loudness


def bell_draw(own_key, shape, width, most, shards=(), kind=jnp.bfloat16):
    factor_of = level_of(own_key, shape, shards, -0.22, 0.18) if shards else 1.0
    entries = jax.random.normal(own_key, shape, jnp.float32) * width * factor_of
    return jnp.minimum(jnp.maximum(entries, -most), most).astype(kind)


def setup_inputs(seed: int = 0) -> dict:
    seeds = jax.random.split(jax.random.key(seed), 4)
    projections = bell_draw(seeds[0], (SEQS, LEN, 3, D), 1.0, 6.0, ((1, 32),))
    impulse = draw_impulse(jax.random.fold_in(seeds[3], 71), 0)
    skip_gain = jnp.clip(jnp.exp(math.log(1.5) - 1.60943787 * jax.random.uniform(seeds[2], (D,), jnp.float32) ** level_of(seeds[2], (D,), ((0, 16),), -0.2, 0.2)), 0.3, 1.5)
    return dict(projections=projections, impulse=impulse, skip_gain=skip_gain)


def forward_table(length):
    frequency = lax.broadcasted_iota(jnp.int32, (length, length), 0)
    sample = lax.broadcasted_iota(jnp.int32, (length, length), 1)
    angles = ((frequency * sample) % (2 * length)).astype(jnp.float32) * (math.pi / length)
    nyquist = jnp.where(sample % 2 == 0, jnp.float32(1.0), jnp.float32(-1.0))
    packed_imag = jnp.where(frequency == 0, nyquist, -jnp.sin(angles))
    return jnp.stack([jnp.cos(angles), packed_imag], axis=0)


def packed_spectrum(samples):
    length = samples.shape[-2]
    spectrum = jnp.fft.rfft(samples, n=2 * length, axis=-2)
    real_rows = jnp.real(spectrum)
    imag_rows = jnp.imag(spectrum)
    packed_imag = jnp.concatenate([real_rows[..., length:, :], imag_rows[..., 1:length, :]], axis=-2)
    return jnp.stack([real_rows[..., :length, :], packed_imag], axis=-3)


def spectral_product(left_side, right_side):
    left_real = left_side[..., 0, :, :]
    left_imag = left_side[..., 1, :, :]
    right_real = right_side[..., 0, :, :]
    right_imag = right_side[..., 1, :, :]
    first_bin = lax.broadcasted_iota(jnp.int32, (left_real.shape[-2], 1), 0) == 0
    real_part = jnp.where(first_bin, left_real * right_real, left_real * right_real - left_imag * right_imag)
    imag_part = jnp.where(first_bin, left_imag * right_imag, left_real * right_imag + left_imag * right_real)
    return jnp.stack([real_part, imag_part], axis=-3)


def inverse_spectrum(packed):
    length = packed.shape[-2]
    nyquist_row = packed[..., 1, :1, :]
    real_rows = jnp.concatenate([packed[..., 0, :, :], nyquist_row], axis=-2)
    imag_rows = jnp.concatenate([jnp.zeros_like(nyquist_row), packed[..., 1, 1:, :], jnp.zeros_like(nyquist_row)], axis=-2)
    return jnp.fft.irfft(real_rows + 1j * imag_rows, n=2 * length, axis=-2)


def reference(projections, impulse, skip_gain):
    blocks = LEN // SPAN
    channel_block = math.gcd(D, 512)
    groups = D // channel_block
    table_low = forward_table(SPAN).astype(jnp.bfloat16)
    gate_rows = projections[:, :, 0, :]
    mixed_input = (projections[:, :, 1, :].astype(jnp.float32) * projections[:, :, 2, :].astype(jnp.float32)).astype(jnp.bfloat16)
    gate_split = gate_rows.reshape(SEQS, LEN, groups, channel_block).transpose(2, 0, 1, 3)
    mixed_split = mixed_input.reshape(SEQS, LEN, groups, channel_block).transpose(2, 0, 1, 3)
    impulse_split = impulse.reshape(LEN, groups, channel_block).transpose(1, 0, 2)
    skip_split = skip_gain.reshape(groups, channel_block)

    def one_group(inputs):
        gate_part, mixed_part, impulse_part, skip_part = inputs
        mixed_wide = lax.optimization_barrier(mixed_part).astype(jnp.float32)
        table_wide = lax.optimization_barrier(table_low).astype(jnp.float32)
        input_spec = jnp.einsum("pkn,sbnc->sbpkc", table_wide, mixed_wide.reshape(SEQS, blocks, SPAN, channel_block), precision=lax.Precision.HIGHEST).astype(jnp.bfloat16)
        input_spec = lax.optimization_barrier(input_spec).astype(jnp.float32)
        filter_spec = packed_spectrum(impulse_part.reshape(blocks, SPAN, channel_block))
        summed_blocks = []
        for target in range(blocks):
            summed = spectral_product(input_spec[:, 0], filter_spec[target])
            for source in range(1, target + 1):
                summed = summed + spectral_product(input_spec[:, source], filter_spec[target - source])
            summed_blocks.append(summed)
        stacked = jnp.stack(summed_blocks, axis=1)
        signal = inverse_spectrum(stacked)
        head_part = signal[:, :, :SPAN]
        tail_part = jnp.concatenate([jnp.zeros_like(signal[:, :1, SPAN:]), signal[:, :-1, SPAN:]], axis=1)
        convolved = (head_part + tail_part).reshape(SEQS, LEN, channel_block) + skip_part * mixed_wide
        return (gate_part.astype(jnp.float32) * convolved).astype(jnp.bfloat16)

    result = lax.map(one_group, (gate_split, mixed_split, impulse_split, skip_split))
    return result.transpose(1, 2, 0, 3).reshape(SEQS, LEN, D)
```

```python
import functools
import math

import jax
import jax.numpy as jnp
from jax import lax
from jax.experimental import pallas as pl
from jax.experimental.pallas import tpu as pltpu
from jax.sharding import PartitionSpec as P
import ml_dtypes
import numpy as np

MESH = pl.DeviceIdType.MESH
LANES = 128


def passed_along(value, axis, steps):
    count = lax.axis_size(axis)
    leading, last = (max(0, -steps), min(count, count - steps))
    return lax.ppermute(value, axis, [(source, source + steps) for source in range(leading, last)])


def forward_table(length):
    frequency = lax.broadcasted_iota(jnp.int32, (length, length), 0)
    sample = lax.broadcasted_iota(jnp.int32, (length, length), 1)
    angles = (frequency * sample % (2 * length)).astype(jnp.float32) * (math.pi / length)
    nyquist = jnp.where(sample % 2 == 0, jnp.float32(1.0), jnp.float32(-1.0))
    packed_imag = jnp.where(frequency == 0, nyquist, -jnp.sin(angles))
    return jnp.stack([jnp.cos(angles), packed_imag], axis=0)


def inverse_table(length):
    sample = lax.broadcasted_iota(jnp.int32, (2 * length, length), 0)
    frequency = lax.broadcasted_iota(jnp.int32, (2 * length, length), 1)
    angles = (frequency * sample % (2 * length)).astype(jnp.float32) * (math.pi / length)
    weight = jnp.where(frequency == 0, jnp.float32(0.5), jnp.float32(1.0)) / length
    nyquist = jnp.where(sample % 2 == 0, jnp.float32(0.5), jnp.float32(-0.5)) / length
    imag_part = jnp.where(frequency == 0, nyquist, -weight * jnp.sin(angles))
    return jnp.stack([weight * jnp.cos(angles), imag_part], axis=1)


def spectral_product(left_side, right_side):
    left_real = left_side[..., 0, :, :]
    left_imag = left_side[..., 1, :, :]
    right_real = right_side[..., 0, :, :]
    right_imag = right_side[..., 1, :, :]
    first_bin = lax.broadcasted_iota(jnp.int32, (left_real.shape[-2], 1), 0) == 0
    real_part = jnp.where(
        first_bin, left_real * right_real, left_real * right_real - left_imag * right_imag
    )
    imag_part = jnp.where(
        first_bin, left_imag * right_imag, left_real * right_imag + left_imag * right_real
    )
    return jnp.stack([real_part, imag_part], axis=-3)


def general_body(projections, impulse, skip_gain):
    length = impulse.shape[0]
    blocks = lax.axis_size("ctx")
    position = lax.axis_index("ctx")
    forward = forward_table(length)
    forward_low = forward.astype(jnp.bfloat16)
    received = lax.all_to_all(projections, "ch", split_axis=3, concat_axis=1, tiled=True)
    gate_part = received[:, :, 0, :]
    mixed_input = (
        received[:, :, 1, :].astype(jnp.float32) * received[:, :, 2, :].astype(jnp.float32)
    ).astype(jnp.bfloat16)
    spectrum, mixed_input, gate_rows = (
        jnp.einsum(
            "pkn,snc->spkc", forward_low, mixed_input, preferred_element_type=jnp.float32
        ).astype(jnp.bfloat16),
        mixed_input,
        gate_part,
    )
    own_filter = jnp.einsum("pkn,nc->pkc", forward, impulse, precision=lax.Precision.HIGHEST)
    filters = lax.all_gather(own_filter[None], "ctx", axis=0, tiled=True)
    zero_carry = jnp.zeros(spectrum.shape, jnp.float32)
    pieces = lax.all_gather(spectrum[None], "ctx", axis=0, tiled=True)
    current = zero_carry
    previous = zero_carry
    for offset in range(pieces.shape[0]):
        source = pieces[offset].astype(jnp.float32)
        lag_index = position - offset
        chosen = lax.dynamic_index_in_dim(
            filters, jnp.clip(lag_index, 0, blocks - 1), 0, keepdims=False
        )
        weight = (lag_index >= 0).astype(jnp.float32)
        current = current + spectral_product(source, chosen) * weight
    current, previous = (current, previous)
    inverse = inverse_table(length)
    signal = jnp.einsum("npk,spkc->snc", inverse, current, precision=lax.Precision.HIGHEST)
    head_part = signal[:, :length]
    tail_part = passed_along(signal[:, length:], "ctx", 1)
    mixed_wide = lax.optimization_barrier(mixed_input).astype(jnp.float32)
    convolved = head_part + tail_part + skip_gain * mixed_wide
    gated = (gate_rows.astype(jnp.float32) * convolved).astype(jnp.bfloat16)
    return lax.all_to_all(gated, "ch", split_axis=1, concat_axis=2, tiled=True)


def split_table(length):
    frequency = np.arange(length)[:, None]
    sample = np.arange(length)[None, :]
    angles = (frequency * sample % (2 * length)) * (math.pi / length)
    nyquist = np.where(sample % 2 == 0, 1.0, -1.0)
    imag = np.where(frequency == 0, nyquist, -np.sin(angles))
    table = np.concatenate([np.cos(angles), imag], axis=0)
    high = table.astype(ml_dtypes.bfloat16)
    low = (table - high.astype(np.float64)).astype(ml_dtypes.bfloat16)
    return high, low


def dot(left, right):
    return jnp.dot(left, right, preferred_element_type=jnp.float32)


def mixer_kernel(
    ctx_size, ch_size,
    proj_ref, impulse_ref, skip_ref, high_ref, low_ref,
    conv_ref,
    kv, mixed, received, result, lags, coef, back_high, back_low, sum_high, sum_low,
    load_sem, lag_sems, out_send, out_recv, home_send, home_recv,
):
    seqs, _, tokens, _ = proj_ref.shape
    span = impulse_ref.shape[0]
    count = ctx_size * ch_size
    y, c = lax.axis_index("ctx"), lax.axis_index("ch")
    me = y * ch_size + c
    tile = 128
    tiles = span // tile

    def place(device):
        return device // ch_size, device % ch_size

    def columns(device):
        py, pc = place(device)
        return pl.ds(pl.multiple_of((pc * ctx_size + py) * LANES, LANES), LANES)

    def rows(device):
        return pl.ds(pl.multiple_of(device * tokens, tokens), tokens)

    def peer(step):
        return lax.rem(me + step, count)

    def load(s):
        return pltpu.make_async_copy(proj_ref.at[s, pl.ds(1, 2)], kv.at[s], load_sem.at[s])

    for s in range(seqs):
        load(s).start()
    own_lag = pltpu.make_async_copy(
        impulse_ref.at[:, pl.ds(pl.multiple_of(y * LANES, LANES), LANES)], lags.at[y], lag_sems.at[0]
    )
    own_lag.start()

    barrier = pltpu.get_barrier_semaphore()

    def greet(step, carry):
        pl.semaphore_signal(barrier, inc=1, device_id=place(peer(step)), device_id_type=MESH)
        return carry

    lax.fori_loop(1, count, greet, 0)
    pl.semaphore_wait(barrier, count - 1)

    other = 1 - y
    lag_copy = pltpu.make_async_remote_copy(
        src_ref=impulse_ref.at[:, pl.ds(pl.multiple_of(other * LANES, LANES), LANES)],
        dst_ref=lags.at[y],
        send_sem=lag_sems.at[1],
        recv_sem=lag_sems.at[2],
        device_id=(other, c),
        device_id_type=MESH,
    )
    lag_copy.start()

    def send_out(s, carry):
        load(s).wait()
        mixed[s] = (kv[s, 0].astype(jnp.float32) * kv[s, 1].astype(jnp.float32)).astype(jnp.bfloat16)
        pltpu.make_async_copy(
            mixed.at[s, :, columns(me)], received.at[s, rows(me), :], out_recv.at[s]
        ).start()

        def one(step, inner):
            target = peer(step)
            pltpu.make_async_remote_copy(
                src_ref=mixed.at[s, :, columns(target)],
                dst_ref=received.at[s, rows(me), :],
                send_sem=out_send.at[s],
                recv_sem=out_recv.at[s],
                device_id=place(target),
                device_id_type=MESH,
            ).start()
            return inner

        return lax.fori_loop(1, count, one, carry)

    lax.fori_loop(0, seqs, send_out, 0)

    row = lax.broadcasted_iota(jnp.int32, (span, span), 0)
    col = lax.broadcasted_iota(jnp.int32, (span, span), 1)
    alternating = jnp.where(row % 2 == 0, jnp.float32(1.0), jnp.float32(-1.0))
    imag = high_ref[span:, :].astype(jnp.float32)
    imag = jnp.where(row == 0, jnp.float32(0.0), imag)
    back_high[:, :span] = high_ref[:span, :]
    back_high[:, span:] = jnp.where(col == 0, alternating, imag).astype(jnp.bfloat16)
    back_low[:, :span] = low_ref[:span, :]
    back_low[:, span:] = low_ref[span:, :]

    own_lag.wait()
    lag_copy.wait()
    taps = jnp.concatenate([lags[0], lags[1]], axis=1)
    taps_high = taps.astype(jnp.bfloat16)
    taps_low = (taps - taps_high.astype(jnp.float32)).astype(jnp.bfloat16)
    for t in range(tiles):
        parts = []
        for p in range(2):
            at = pl.ds(p * span + t * tile, tile)
            parts.append(
                dot(high_ref[at, :], taps_high)
                + dot(high_ref[at, :], taps_low)
                + dot(low_ref[at, :], taps_high)
            )
        real, imag = parts
        bins = lax.broadcasted_iota(jnp.int32, (tile, LANES), 0) + t * tile
        first = bins == 0
        sign = jnp.where(bins % 2 == 0, jnp.float32(1.0), jnp.float32(-1.0))
        weight = jnp.where(first, jnp.float32(0.5 / span), jnp.float32(1.0 / span))
        re0, im0 = real[:, :LANES] * weight, imag[:, :LANES] * weight
        re1 = real[:, LANES:] * weight + sign * re0
        im1 = imag[:, LANES:] * weight + sign * im0
        at = pl.ds(t * tile, tile)
        for base, re, im in ((0, re0, im0), (3, re1, im1)):
            coef[base, at, :] = re
            coef[base + 1, at, :] = jnp.where(first, jnp.float32(0.0), im)
            coef[base + 2, at, :] = jnp.where(first, im, re)

    def convolve(s, carry):
        pltpu.make_async_copy(received.at[s], received.at[s], out_recv.at[s]).wait()
        signal = jnp.concatenate([received[s, :span, :], received[s, span:, :]], axis=1)
        for t in range(tiles):
            at = pl.ds(t * tile, tile)
            re = dot(high_ref[at, :], signal).astype(jnp.bfloat16).astype(jnp.float32)
            im = dot(high_ref[pl.ds(span + t * tile, tile), :], signal)
            im = im.astype(jnp.bfloat16).astype(jnp.float32)
            re0, re1 = re[:, :LANES], re[:, LANES:]
            im0, im1 = im[:, :LANES], im[:, LANES:]
            a0, b0, c0 = coef[0, at, :], coef[1, at, :], coef[2, at, :]
            a1, b1, c1 = coef[3, at, :], coef[4, at, :], coef[5, at, :]
            sums = (
                (re0 * a0 - im0 * b0, im0 * c0 + re0 * b0),
                (
                    re0 * a1 - im0 * b1 + (re1 * a0 - im1 * b0),
                    im0 * c1 + re0 * b1 + (im1 * c0 + re1 * b0),
                ),
            )
            for p in range(2):
                total = jnp.concatenate([sums[0][p], sums[1][p]], axis=1)
                high = total.astype(jnp.bfloat16)
                into = pl.ds(p * span + t * tile, tile)
                sum_high[into, :] = high
                sum_low[into, :] = (total - high.astype(jnp.float32)).astype(jnp.bfloat16)
        gain = skip_ref[pl.ds(y, 1), :]
        for t in range(tiles):
            at = pl.ds(t * tile, tile)
            response = (
                dot(back_high[at, :], sum_high[...])
                + dot(back_high[at, :], sum_low[...])
                + dot(back_low[at, :], sum_high[...])
            )
            for j in range(2):
                into = pl.ds(j * span + t * tile, tile)
                direct = gain * received[s, into, :].astype(jnp.float32)
                result[s, into, :] = (
                    response[:, j * LANES : (j + 1) * LANES] + direct
                ).astype(jnp.bfloat16)
        pltpu.make_async_copy(
            result.at[s, rows(me), :], conv_ref.at[s, :, columns(me)], home_recv.at[s]
        ).start()

        def one(step, inner):
            target = peer(step)
            pltpu.make_async_remote_copy(
                src_ref=result.at[s, rows(target), :],
                dst_ref=conv_ref.at[s, :, columns(me)],
                send_sem=home_send.at[s],
                recv_sem=home_recv.at[s],
                device_id=place(target),
                device_id_type=MESH,
            ).start()
            return inner

        return lax.fori_loop(1, count, one, carry)

    lax.fori_loop(0, seqs, convolve, 0)

    def drain(s, carry):
        sent = received.at[s, pl.ds(0, (count - 1) * tokens), :]
        pltpu.make_async_copy(sent, sent, out_send.at[s]).wait()
        pltpu.make_async_copy(sent, sent, home_send.at[s]).wait()
        pltpu.make_async_copy(conv_ref.at[s], conv_ref.at[s], home_recv.at[s]).wait()
        return carry

    lax.fori_loop(0, seqs, drain, 0)


def split_body(projections, impulse, skip_gain):
    ctx_size, ch_size = lax.axis_size("ctx"), lax.axis_size("ch")
    seqs, tokens, _, width = projections.shape
    span = impulse.shape[0]
    length = ctx_size * ch_size * tokens
    high, low = split_table(span)
    features = jnp.transpose(projections, (0, 2, 1, 3))
    anywhere = pl.BlockSpec(memory_space=pl.ANY)
    vmem = pl.BlockSpec(memory_space=pltpu.VMEM)
    bf16, f32 = jnp.bfloat16, jnp.float32
    convolved = pl.pallas_call(
        functools.partial(mixer_kernel, ctx_size, ch_size),
        out_shape=jax.ShapeDtypeStruct((seqs, tokens, width), bf16),
        in_specs=[anywhere, anywhere, vmem, vmem, vmem],
        out_specs=anywhere,
        scratch_shapes=[
            pltpu.VMEM((seqs, 2, tokens, width), bf16),
            pltpu.VMEM((seqs, tokens, width), bf16),
            pltpu.VMEM((seqs, length, LANES), bf16),
            pltpu.VMEM((seqs, length, LANES), bf16),
            pltpu.VMEM((2, span, LANES), f32),
            pltpu.VMEM((6, span, LANES), f32),
            pltpu.VMEM((span, 2 * span), bf16),
            pltpu.VMEM((span, 2 * span), bf16),
            pltpu.VMEM((2 * span, 2 * LANES), bf16),
            pltpu.VMEM((2 * span, 2 * LANES), bf16),
            pltpu.SemaphoreType.DMA((seqs,)),
            pltpu.SemaphoreType.DMA((3,)),
            pltpu.SemaphoreType.DMA((seqs,)),
            pltpu.SemaphoreType.DMA((seqs,)),
            pltpu.SemaphoreType.DMA((seqs,)),
            pltpu.SemaphoreType.DMA((seqs,)),
        ],
        compiler_params=pltpu.CompilerParams(
            collective_id=0, has_side_effects=True, vmem_limit_bytes=40 * 1024 * 1024
        ),
    )(features, impulse, skip_gain.reshape(2, LANES), jnp.asarray(high), jnp.asarray(low))
    gate = features[:, 0]
    return (gate.astype(f32) * convolved.astype(f32)).astype(bf16)


def body(projections, impulse, skip_gain):
    ctx_size = lax.axis_size("ctx")
    whole_tiles = projections.shape[1] % 16 == 0 and impulse.shape[0] % 256 == 0
    if ctx_size == 2 and impulse.shape[1] == 2 * LANES and whole_tiles:
        return split_body(projections, impulse, skip_gain)
    return general_body(projections, impulse, skip_gain)


def solution(mesh):
    return jax.shard_map(
        body,
        mesh=mesh,
        in_specs=(P(None, ("ctx", "ch"), None, None), P("ctx", "ch"), P("ch")),
        out_specs=P(None, ("ctx", "ch"), None),
        check_vma=False,
    )
```

```python
import functools
import math

import jax
import jax.numpy as jnp
from jax import lax
from jax.experimental import pallas as pl
from jax.experimental.pallas import tpu as pltpu
from jax.sharding import PartitionSpec as P
import ml_dtypes
import numpy as np

MESH = pl.DeviceIdType.MESH
LANES = 128


def passed_along(value, axis, steps):
    count = lax.axis_size(axis)
    leading, last = (max(0, -steps), min(count, count - steps))
    return lax.ppermute(value, axis, [(source, source + steps) for source in range(leading, last)])


def forward_table(length):
    frequency = lax.broadcasted_iota(jnp.int32, (length, length), 0)
    sample = lax.broadcasted_iota(jnp.int32, (length, length), 1)
    angles = (frequency * sample % (2 * length)).astype(jnp.float32) * (math.pi / length)
    nyquist = jnp.where(sample % 2 == 0, jnp.float32(1.0), jnp.float32(-1.0))
    packed_imag = jnp.where(frequency == 0, nyquist, -jnp.sin(angles))
    return jnp.stack([jnp.cos(angles), packed_imag], axis=0)


def inverse_table(length):
    sample = lax.broadcasted_iota(jnp.int32, (2 * length, length), 0)
    frequency = lax.broadcasted_iota(jnp.int32, (2 * length, length), 1)
    angles = (frequency * sample % (2 * length)).astype(jnp.float32) * (math.pi / length)
    weight = jnp.where(frequency == 0, jnp.float32(0.5), jnp.float32(1.0)) / length
    nyquist = jnp.where(sample % 2 == 0, jnp.float32(0.5), jnp.float32(-0.5)) / length
    imag_part = jnp.where(frequency == 0, nyquist, -weight * jnp.sin(angles))
    return jnp.stack([weight * jnp.cos(angles), imag_part], axis=1)


def spectral_product(left_side, right_side):
    left_real = left_side[..., 0, :, :]
    left_imag = left_side[..., 1, :, :]
    right_real = right_side[..., 0, :, :]
    right_imag = right_side[..., 1, :, :]
    first_bin = lax.broadcasted_iota(jnp.int32, (left_real.shape[-2], 1), 0) == 0
    real_part = jnp.where(
        first_bin, left_real * right_real, left_real * right_real - left_imag * right_imag
    )
    imag_part = jnp.where(
        first_bin, left_imag * right_imag, left_real * right_imag + left_imag * right_real
    )
    return jnp.stack([real_part, imag_part], axis=-3)


def general_body(projections, impulse, skip_gain):
    length = impulse.shape[0]
    blocks = lax.axis_size("ctx")
    position = lax.axis_index("ctx")
    forward = forward_table(length)
    forward_low = forward.astype(jnp.bfloat16)
    received = lax.all_to_all(projections, "ch", split_axis=3, concat_axis=1, tiled=True)
    gate_part = received[:, :, 0, :]
    mixed_input = (
        received[:, :, 1, :].astype(jnp.float32) * received[:, :, 2, :].astype(jnp.float32)
    ).astype(jnp.bfloat16)
    spectrum, mixed_input, gate_rows = (
        jnp.einsum(
            "pkn,snc->spkc", forward_low, mixed_input, preferred_element_type=jnp.float32
        ).astype(jnp.bfloat16),
        mixed_input,
        gate_part,
    )
    own_filter = jnp.einsum("pkn,nc->pkc", forward, impulse, precision=lax.Precision.HIGHEST)
    filters = lax.all_gather(own_filter[None], "ctx", axis=0, tiled=True)
    zero_carry = jnp.zeros(spectrum.shape, jnp.float32)
    pieces = lax.all_gather(spectrum[None], "ctx", axis=0, tiled=True)
    current = zero_carry
    previous = zero_carry
    for offset in range(pieces.shape[0]):
        source = pieces[offset].astype(jnp.float32)
        lag_index = position - offset
        chosen = lax.dynamic_index_in_dim(
            filters, jnp.clip(lag_index, 0, blocks - 1), 0, keepdims=False
        )
        weight = (lag_index >= 0).astype(jnp.float32)
        current = current + spectral_product(source, chosen) * weight
    current, previous = (current, previous)
    inverse = inverse_table(length)
    signal = jnp.einsum("npk,spkc->snc", inverse, current, precision=lax.Precision.HIGHEST)
    head_part = signal[:, :length]
    tail_part = passed_along(signal[:, length:], "ctx", 1)
    mixed_wide = lax.optimization_barrier(mixed_input).astype(jnp.float32)
    convolved = head_part + tail_part + skip_gain * mixed_wide
    gated = (gate_rows.astype(jnp.float32) * convolved).astype(jnp.bfloat16)
    return lax.all_to_all(gated, "ch", split_axis=1, concat_axis=2, tiled=True)


def split_table(length):
    frequency = np.arange(length)[:, None]
    sample = np.arange(length)[None, :]
    angles = (frequency * sample % (2 * length)) * (math.pi / length)
    nyquist = np.where(sample % 2 == 0, 1.0, -1.0)
    imag = np.where(frequency == 0, nyquist, -np.sin(angles))
    table = np.concatenate([np.cos(angles), imag], axis=0)
    high = table.astype(ml_dtypes.bfloat16)
    low = (table - high.astype(np.float64)).astype(ml_dtypes.bfloat16)
    return high, low


def dot(left, right):
    return jnp.dot(left, right, preferred_element_type=jnp.float32)


def mixer_kernel(
    ctx_size, ch_size,
    proj_ref, impulse_ref, skip_ref, high_hbm, low_hbm,
    conv_ref,
    high_ref, low_ref,    kv, mixed, received, result, lags, coef, back_high, back_low, sum_high, sum_low,
    load_sem, table_sems, lag_sems, out_send, out_recv, home_send, home_recv,
):
    seqs, _, tokens, _ = proj_ref.shape
    span = impulse_ref.shape[0]
    count = ctx_size * ch_size
    y, c = lax.axis_index("ctx"), lax.axis_index("ch")
    me = y * ch_size + c
    tile = 128
    several = 2 if seqs % 2 == 0 else 1
    groups = seqs // several
    tiles = span // tile

    def place(device):
        return device // ch_size, device % ch_size

    def columns(device):
        py, pc = place(device)
        return pl.ds(pl.multiple_of((pc * ctx_size + py) * LANES, LANES), LANES)

    def rows(device):
        return pl.ds(pl.multiple_of(device * tokens, tokens), tokens)

    def peer(step):
        return lax.rem(me + step, count)

    def group(g):
        return pl.ds(g * several, several)

    def load(s):
        return pltpu.make_async_copy(proj_ref.at[s, pl.ds(1, 2)], kv.at[s], load_sem.at[s])

    barrier = pltpu.get_barrier_semaphore()

    def greet(step, carry):
        pl.semaphore_signal(barrier, inc=1, device_id=place(peer(step)), device_id_type=MESH)
        return carry

    lax.fori_loop(1, count, greet, 0)

    for s in range(seqs):
        load(s).start()
    own_lag = pltpu.make_async_copy(
        impulse_ref.at[:, pl.ds(pl.multiple_of(y * LANES, LANES), LANES)], lags.at[y], lag_sems.at[0]
    )
    own_lag.start()
    tables = [
        pltpu.make_async_copy(source, target, table_sems.at[i])
        for i, (source, target) in enumerate(((high_hbm, high_ref), (low_hbm, low_ref)))
    ]
    for table in tables:
        table.start()

    def multiply(s, carry):
        load(s).wait()
        mixed[s] = (kv[s, 0].astype(jnp.float32) * kv[s, 1].astype(jnp.float32)).astype(jnp.bfloat16)
        return carry

    lax.fori_loop(0, seqs, multiply, 0)

    pl.semaphore_wait(barrier, count - 1)

    other = 1 - y
    lag_copy = pltpu.make_async_remote_copy(
        src_ref=impulse_ref.at[:, pl.ds(pl.multiple_of(other * LANES, LANES), LANES)],
        dst_ref=lags.at[y],
        send_sem=lag_sems.at[1],
        recv_sem=lag_sems.at[2],
        device_id=(other, c),
        device_id_type=MESH,
    )
    def send_out(g, carry):
        pltpu.make_async_copy(
            mixed.at[group(g), :, columns(me)], received.at[group(g), rows(me), :], out_recv.at[g]
        ).start()

        def one(step, inner):
            target = peer(step)
            pltpu.make_async_remote_copy(
                src_ref=mixed.at[group(g), :, columns(target)],
                dst_ref=received.at[group(g), rows(me), :],
                send_sem=out_send.at[g],
                recv_sem=out_recv.at[g],
                device_id=place(target),
                device_id_type=MESH,
            ).start()
            return inner

        return lax.fori_loop(1, count, one, carry)

    send_out(0, 0)
    lag_copy.start()
    lax.fori_loop(1, groups, send_out, 0)
    for table in tables:
        table.wait()

    row = lax.broadcasted_iota(jnp.int32, (span, span), 0)
    col = lax.broadcasted_iota(jnp.int32, (span, span), 1)
    alternating = jnp.where(row % 2 == 0, jnp.float32(1.0), jnp.float32(-1.0))
    imag = high_ref[span:, :].astype(jnp.float32)
    imag = jnp.where(row == 0, jnp.float32(0.0), imag)
    back_high[:, :span] = high_ref[:span, :]
    back_high[:, span:] = jnp.where(col == 0, alternating, imag).astype(jnp.bfloat16)
    back_low[:, :span] = low_ref[:span, :]
    back_low[:, span:] = low_ref[span:, :]

    own_lag.wait()
    lag_copy.wait()
    taps = jnp.concatenate([lags[0], lags[1]], axis=1)
    taps_high = taps.astype(jnp.bfloat16)
    taps_low = (taps - taps_high.astype(jnp.float32)).astype(jnp.bfloat16)
    for t in range(tiles):
        parts = []
        for p in range(2):
            at = pl.ds(p * span + t * tile, tile)
            parts.append(
                dot(high_ref[at, :], taps_high)
                + dot(high_ref[at, :], taps_low)
                + dot(low_ref[at, :], taps_high)
            )
        real, imag = parts
        bins = lax.broadcasted_iota(jnp.int32, (tile, LANES), 0) + t * tile
        first = bins == 0
        sign = jnp.where(bins % 2 == 0, jnp.float32(1.0), jnp.float32(-1.0))
        weight = jnp.where(first, jnp.float32(0.5 / span), jnp.float32(1.0 / span))
        re0, im0 = real[:, :LANES] * weight, imag[:, :LANES] * weight
        re1 = real[:, LANES:] * weight + sign * re0
        im1 = imag[:, LANES:] * weight + sign * im0
        at = pl.ds(t * tile, tile)
        for base, re, im in ((0, re0, im0), (3, re1, im1)):
            coef[base, at, :] = re
            coef[base + 1, at, :] = jnp.where(first, jnp.float32(0.0), im)
            coef[base + 2, at, :] = jnp.where(first, im, re)

    def convolve(s, carry):
        signal = jnp.concatenate([received[s, :span, :], received[s, span:, :]], axis=1)
        for t in range(tiles):
            at = pl.ds(t * tile, tile)
            re = dot(high_ref[at, :], signal).astype(jnp.bfloat16).astype(jnp.float32)
            im = dot(high_ref[pl.ds(span + t * tile, tile), :], signal)
            im = im.astype(jnp.bfloat16).astype(jnp.float32)
            re0, re1 = re[:, :LANES], re[:, LANES:]
            im0, im1 = im[:, :LANES], im[:, LANES:]
            a0, b0, c0 = coef[0, at, :], coef[1, at, :], coef[2, at, :]
            a1, b1, c1 = coef[3, at, :], coef[4, at, :], coef[5, at, :]
            sums = (
                (re0 * a0 - im0 * b0, im0 * c0 + re0 * b0),
                (
                    re0 * a1 - im0 * b1 + (re1 * a0 - im1 * b0),
                    im0 * c1 + re0 * b1 + (im1 * c0 + re1 * b0),
                ),
            )
            for p in range(2):
                total = jnp.concatenate([sums[0][p], sums[1][p]], axis=1)
                high = total.astype(jnp.bfloat16)
                into = pl.ds(p * span + t * tile, tile)
                sum_high[into, :] = high
                sum_low[into, :] = (total - high.astype(jnp.float32)).astype(jnp.bfloat16)
        gain = skip_ref[pl.ds(y, 1), :]
        for t in range(tiles):
            at = pl.ds(t * tile, tile)
            response = (
                dot(back_high[at, :], sum_high[...])
                + dot(back_high[at, :], sum_low[...])
                + dot(back_low[at, :], sum_high[...])
            )
            for j in range(2):
                into = pl.ds(j * span + t * tile, tile)
                direct = gain * received[s, into, :].astype(jnp.float32)
                result[s, into, :] = (
                    response[:, j * LANES : (j + 1) * LANES] + direct
                ).astype(jnp.bfloat16)
        return carry

    def send_home(g, carry):
        landed = received.at[group(g)]
        pltpu.make_async_copy(landed, landed, out_recv.at[g]).wait()
        lax.fori_loop(g * several, (g + 1) * several, convolve, carry)
        pltpu.make_async_copy(
            result.at[group(g), rows(me), :], conv_ref.at[group(g), :, columns(me)], home_recv.at[g]
        ).start()

        def one(step, inner):
            target = peer(step)
            pltpu.make_async_remote_copy(
                src_ref=result.at[group(g), rows(target), :],
                dst_ref=conv_ref.at[group(g), :, columns(me)],
                send_sem=home_send.at[g],
                recv_sem=home_recv.at[g],
                device_id=place(target),
                device_id_type=MESH,
            ).start()
            return inner

        return lax.fori_loop(1, count, one, carry)

    lax.fori_loop(0, groups, send_home, 0)

    def drain(g, carry):
        sent = received.at[group(g), pl.ds(0, (count - 1) * tokens), :]
        home = conv_ref.at[group(g)]
        pltpu.make_async_copy(sent, sent, out_send.at[g]).wait()
        pltpu.make_async_copy(sent, sent, home_send.at[g]).wait()
        pltpu.make_async_copy(home, home, home_recv.at[g]).wait()
        return carry

    lax.fori_loop(0, groups, drain, 0)


def split_body(projections, impulse, skip_gain):
    ctx_size, ch_size = lax.axis_size("ctx"), lax.axis_size("ch")
    seqs, tokens, _, width = projections.shape
    span = impulse.shape[0]
    length = ctx_size * ch_size * tokens
    high, low = split_table(span)
    features = jnp.transpose(projections, (0, 2, 1, 3))
    anywhere = pl.BlockSpec(memory_space=pl.ANY)
    hbm = pl.BlockSpec(memory_space=pltpu.HBM)
    vmem = pl.BlockSpec(memory_space=pltpu.VMEM)
    bf16, f32 = jnp.bfloat16, jnp.float32
    convolved = pl.pallas_call(
        functools.partial(mixer_kernel, ctx_size, ch_size),
        out_shape=jax.ShapeDtypeStruct((seqs, tokens, width), bf16),
        in_specs=[hbm, hbm, vmem, hbm, hbm],
        out_specs=anywhere,
        scratch_shapes=[
            pltpu.VMEM((2 * span, span), bf16),
            pltpu.VMEM((2 * span, span), bf16),
            pltpu.VMEM((seqs, 2, tokens, width), bf16),
            pltpu.VMEM((seqs, tokens, width), bf16),
            pltpu.VMEM((seqs, length, LANES), bf16),
            pltpu.VMEM((seqs, length, LANES), bf16),
            pltpu.VMEM((2, span, LANES), f32),
            pltpu.VMEM((6, span, LANES), f32),
            pltpu.VMEM((span, 2 * span), bf16),
            pltpu.VMEM((span, 2 * span), bf16),
            pltpu.VMEM((2 * span, 2 * LANES), bf16),
            pltpu.VMEM((2 * span, 2 * LANES), bf16),
            pltpu.SemaphoreType.DMA((seqs,)),
            pltpu.SemaphoreType.DMA((2,)),
            pltpu.SemaphoreType.DMA((3,)),
            pltpu.SemaphoreType.DMA((seqs,)),
            pltpu.SemaphoreType.DMA((seqs,)),
            pltpu.SemaphoreType.DMA((seqs,)),
            pltpu.SemaphoreType.DMA((seqs,)),
        ],
        compiler_params=pltpu.CompilerParams(
            collective_id=0, has_side_effects=True, vmem_limit_bytes=60 * 1024 * 1024
        ),
    )(features, impulse, skip_gain.reshape(2, LANES), jnp.asarray(high), jnp.asarray(low))
    gate = features[:, 0]
    return (gate.astype(f32) * convolved.astype(f32)).astype(bf16)


def body(projections, impulse, skip_gain):
    ctx_size = lax.axis_size("ctx")
    whole_tiles = projections.shape[1] % 16 == 0 and impulse.shape[0] % 256 == 0
    if ctx_size == 2 and impulse.shape[1] == 2 * LANES and whole_tiles:
        return split_body(projections, impulse, skip_gain)
    return general_body(projections, impulse, skip_gain)


def solution(mesh):
    return jax.shard_map(
        body,
        mesh=mesh,
        in_specs=(P(None, ("ctx", "ch"), None, None), P("ctx", "ch"), P("ch")),
        out_specs=P(None, ("ctx", "ch"), None),
        check_vma=False,
    )
```

```python
import functools
import math

import jax
import jax.numpy as jnp
from jax import lax
from jax.experimental import pallas as pl
from jax.experimental.pallas import tpu as pltpu
from jax.sharding import PartitionSpec as P
import ml_dtypes
import numpy as np

MESH = pl.DeviceIdType.MESH
LANES = 128


def passed_along(value, axis, steps):
    count = lax.axis_size(axis)
    leading, last = (max(0, -steps), min(count, count - steps))
    return lax.ppermute(value, axis, [(source, source + steps) for source in range(leading, last)])


def forward_table(length):
    frequency = lax.broadcasted_iota(jnp.int32, (length, length), 0)
    sample = lax.broadcasted_iota(jnp.int32, (length, length), 1)
    angles = (frequency * sample % (2 * length)).astype(jnp.float32) * (math.pi / length)
    nyquist = jnp.where(sample % 2 == 0, jnp.float32(1.0), jnp.float32(-1.0))
    packed_imag = jnp.where(frequency == 0, nyquist, -jnp.sin(angles))
    return jnp.stack([jnp.cos(angles), packed_imag], axis=0)


def inverse_table(length):
    sample = lax.broadcasted_iota(jnp.int32, (2 * length, length), 0)
    frequency = lax.broadcasted_iota(jnp.int32, (2 * length, length), 1)
    angles = (frequency * sample % (2 * length)).astype(jnp.float32) * (math.pi / length)
    weight = jnp.where(frequency == 0, jnp.float32(0.5), jnp.float32(1.0)) / length
    nyquist = jnp.where(sample % 2 == 0, jnp.float32(0.5), jnp.float32(-0.5)) / length
    imag_part = jnp.where(frequency == 0, nyquist, -weight * jnp.sin(angles))
    return jnp.stack([weight * jnp.cos(angles), imag_part], axis=1)


def spectral_product(left_side, right_side):
    left_real = left_side[..., 0, :, :]
    left_imag = left_side[..., 1, :, :]
    right_real = right_side[..., 0, :, :]
    right_imag = right_side[..., 1, :, :]
    first_bin = lax.broadcasted_iota(jnp.int32, (left_real.shape[-2], 1), 0) == 0
    real_part = jnp.where(
        first_bin, left_real * right_real, left_real * right_real - left_imag * right_imag
    )
    imag_part = jnp.where(
        first_bin, left_imag * right_imag, left_real * right_imag + left_imag * right_real
    )
    return jnp.stack([real_part, imag_part], axis=-3)


def general_body(projections, impulse, skip_gain):
    length = impulse.shape[0]
    blocks = lax.axis_size("ctx")
    position = lax.axis_index("ctx")
    forward = forward_table(length)
    forward_low = forward.astype(jnp.bfloat16)
    received = lax.all_to_all(projections, "ch", split_axis=3, concat_axis=1, tiled=True)
    gate_part = received[:, :, 0, :]
    mixed_input = (
        received[:, :, 1, :].astype(jnp.float32) * received[:, :, 2, :].astype(jnp.float32)
    ).astype(jnp.bfloat16)
    spectrum, mixed_input, gate_rows = (
        jnp.einsum(
            "pkn,snc->spkc", forward_low, mixed_input, preferred_element_type=jnp.float32
        ).astype(jnp.bfloat16),
        mixed_input,
        gate_part,
    )
    own_filter = jnp.einsum("pkn,nc->pkc", forward, impulse, precision=lax.Precision.HIGHEST)
    filters = lax.all_gather(own_filter[None], "ctx", axis=0, tiled=True)
    zero_carry = jnp.zeros(spectrum.shape, jnp.float32)
    pieces = lax.all_gather(spectrum[None], "ctx", axis=0, tiled=True)
    current = zero_carry
    previous = zero_carry
    for offset in range(pieces.shape[0]):
        source = pieces[offset].astype(jnp.float32)
        lag_index = position - offset
        chosen = lax.dynamic_index_in_dim(
            filters, jnp.clip(lag_index, 0, blocks - 1), 0, keepdims=False
        )
        weight = (lag_index >= 0).astype(jnp.float32)
        current = current + spectral_product(source, chosen) * weight
    current, previous = (current, previous)
    inverse = inverse_table(length)
    signal = jnp.einsum("npk,spkc->snc", inverse, current, precision=lax.Precision.HIGHEST)
    head_part = signal[:, :length]
    tail_part = passed_along(signal[:, length:], "ctx", 1)
    mixed_wide = lax.optimization_barrier(mixed_input).astype(jnp.float32)
    convolved = head_part + tail_part + skip_gain * mixed_wide
    gated = (gate_rows.astype(jnp.float32) * convolved).astype(jnp.bfloat16)
    return lax.all_to_all(gated, "ch", split_axis=1, concat_axis=2, tiled=True)


def split_table(length):
    frequency = np.arange(length)[:, None]
    sample = np.arange(length)[None, :]
    angles = (frequency * sample % (2 * length)) * (math.pi / length)
    nyquist = np.where(sample % 2 == 0, 1.0, -1.0)
    imag = np.where(frequency == 0, nyquist, -np.sin(angles))
    table = np.concatenate([np.cos(angles), imag], axis=0)
    high = table.astype(ml_dtypes.bfloat16)
    low = (table - high.astype(np.float64)).astype(ml_dtypes.bfloat16)
    return high, low


def dot(left, right):
    return jnp.dot(left, right, preferred_element_type=jnp.float32)


def mixer_kernel(
    ctx_size, ch_size,
    proj_ref, impulse_ref, skip_ref, high_hbm, low_hbm,
    gated_ref,
    high_ref, low_ref,    kv, gate, conv_ref, mixed, received, result, lags, coef, back_high, back_low, sum_high, sum_low,
    load_sem, gate_sem, store_sem, table_sems, lag_sems, out_send, out_recv, home_send, home_recv,
):
    seqs, _, tokens, _ = proj_ref.shape
    span = impulse_ref.shape[0]
    count = ctx_size * ch_size
    y, c = lax.axis_index("ctx"), lax.axis_index("ch")
    me = y * ch_size + c
    tile = 128
    several = 2 if seqs % 2 == 0 else 1
    groups = seqs // several
    tiles = span // tile

    def place(device):
        return device // ch_size, device % ch_size

    def columns(device):
        py, pc = place(device)
        return pl.ds(pl.multiple_of((pc * ctx_size + py) * LANES, LANES), LANES)

    def rows(device):
        return pl.ds(pl.multiple_of(device * tokens, tokens), tokens)

    def peer(step):
        return lax.rem(me + step, count)

    def group(g):
        return pl.ds(g * several, several)

    def load(s):
        return pltpu.make_async_copy(proj_ref.at[s, pl.ds(1, 2)], kv.at[s], load_sem.at[s])

    barrier = pltpu.get_barrier_semaphore()

    def greet(step, carry):
        pl.semaphore_signal(barrier, inc=1, device_id=place(peer(step)), device_id_type=MESH)
        return carry

    lax.fori_loop(1, count, greet, 0)

    for s in range(seqs):
        load(s).start()
    gate_load = pltpu.make_async_copy(proj_ref.at[:, 0], gate, gate_sem)
    own_lag = pltpu.make_async_copy(
        impulse_ref.at[:, pl.ds(pl.multiple_of(y * LANES, LANES), LANES)], lags.at[y], lag_sems.at[0]
    )
    own_lag.start()
    tables = [
        pltpu.make_async_copy(source, target, table_sems.at[i])
        for i, (source, target) in enumerate(((high_hbm, high_ref), (low_hbm, low_ref)))
    ]
    for table in tables:
        table.start()
    gate_load.start()

    def multiply(s, carry):
        load(s).wait()
        mixed[s] = (kv[s, 0].astype(jnp.float32) * kv[s, 1].astype(jnp.float32)).astype(jnp.bfloat16)
        return carry

    lax.fori_loop(0, seqs, multiply, 0)

    pl.semaphore_wait(barrier, count - 1)

    other = 1 - y
    lag_copy = pltpu.make_async_remote_copy(
        src_ref=impulse_ref.at[:, pl.ds(pl.multiple_of(other * LANES, LANES), LANES)],
        dst_ref=lags.at[y],
        send_sem=lag_sems.at[1],
        recv_sem=lag_sems.at[2],
        device_id=(other, c),
        device_id_type=MESH,
    )
    def send_out(g, carry):
        pltpu.make_async_copy(
            mixed.at[group(g), :, columns(me)], received.at[group(g), rows(me), :], out_recv.at[g]
        ).start()

        def one(step, inner):
            target = peer(step)
            pltpu.make_async_remote_copy(
                src_ref=mixed.at[group(g), :, columns(target)],
                dst_ref=received.at[group(g), rows(me), :],
                send_sem=out_send.at[g],
                recv_sem=out_recv.at[g],
                device_id=place(target),
                device_id_type=MESH,
            ).start()
            return inner

        return lax.fori_loop(1, count, one, carry)

    send_out(0, 0)
    lag_copy.start()
    lax.fori_loop(1, groups, send_out, 0)
    for table in tables:
        table.wait()

    row = lax.broadcasted_iota(jnp.int32, (span, span), 0)
    col = lax.broadcasted_iota(jnp.int32, (span, span), 1)
    alternating = jnp.where(row % 2 == 0, jnp.float32(1.0), jnp.float32(-1.0))
    imag = high_ref[span:, :].astype(jnp.float32)
    imag = jnp.where(row == 0, jnp.float32(0.0), imag)
    back_high[:, :span] = high_ref[:span, :]
    back_high[:, span:] = jnp.where(col == 0, alternating, imag).astype(jnp.bfloat16)
    back_low[:, :span] = low_ref[:span, :]
    back_low[:, span:] = low_ref[span:, :]

    own_lag.wait()
    lag_copy.wait()
    taps = jnp.concatenate([lags[0], lags[1]], axis=1)
    taps_high = taps.astype(jnp.bfloat16)
    taps_low = (taps - taps_high.astype(jnp.float32)).astype(jnp.bfloat16)
    for t in range(tiles):
        parts = []
        for p in range(2):
            at = pl.ds(p * span + t * tile, tile)
            parts.append(
                dot(high_ref[at, :], taps_high)
                + dot(high_ref[at, :], taps_low)
                + dot(low_ref[at, :], taps_high)
            )
        real, imag = parts
        bins = lax.broadcasted_iota(jnp.int32, (tile, LANES), 0) + t * tile
        first = bins == 0
        sign = jnp.where(bins % 2 == 0, jnp.float32(1.0), jnp.float32(-1.0))
        weight = jnp.where(first, jnp.float32(0.5 / span), jnp.float32(1.0 / span))
        re0, im0 = real[:, :LANES] * weight, imag[:, :LANES] * weight
        re1 = real[:, LANES:] * weight + sign * re0
        im1 = imag[:, LANES:] * weight + sign * im0
        at = pl.ds(t * tile, tile)
        for base, re, im in ((0, re0, im0), (3, re1, im1)):
            coef[base, at, :] = re
            coef[base + 1, at, :] = jnp.where(first, jnp.float32(0.0), im)
            coef[base + 2, at, :] = jnp.where(first, im, re)

    def convolve(s, carry):
        signal = jnp.concatenate([received[s, :span, :], received[s, span:, :]], axis=1)
        for t in range(tiles):
            at = pl.ds(t * tile, tile)
            re = dot(high_ref[at, :], signal).astype(jnp.bfloat16).astype(jnp.float32)
            im = dot(high_ref[pl.ds(span + t * tile, tile), :], signal)
            im = im.astype(jnp.bfloat16).astype(jnp.float32)
            re0, re1 = re[:, :LANES], re[:, LANES:]
            im0, im1 = im[:, :LANES], im[:, LANES:]
            a0, b0, c0 = coef[0, at, :], coef[1, at, :], coef[2, at, :]
            a1, b1, c1 = coef[3, at, :], coef[4, at, :], coef[5, at, :]
            sums = (
                (re0 * a0 - im0 * b0, im0 * c0 + re0 * b0),
                (
                    re0 * a1 - im0 * b1 + (re1 * a0 - im1 * b0),
                    im0 * c1 + re0 * b1 + (im1 * c0 + re1 * b0),
                ),
            )
            for p in range(2):
                total = jnp.concatenate([sums[0][p], sums[1][p]], axis=1)
                high = total.astype(jnp.bfloat16)
                into = pl.ds(p * span + t * tile, tile)
                sum_high[into, :] = high
                sum_low[into, :] = (total - high.astype(jnp.float32)).astype(jnp.bfloat16)
        gain = skip_ref[pl.ds(y, 1), :]
        for t in range(tiles):
            at = pl.ds(t * tile, tile)
            response = (
                dot(back_high[at, :], sum_high[...])
                + dot(back_high[at, :], sum_low[...])
                + dot(back_low[at, :], sum_high[...])
            )
            for j in range(2):
                into = pl.ds(j * span + t * tile, tile)
                direct = gain * received[s, into, :].astype(jnp.float32)
                result[s, into, :] = (
                    response[:, j * LANES : (j + 1) * LANES] + direct
                ).astype(jnp.bfloat16)
        return carry

    def send_home(g, carry):
        landed = received.at[group(g)]
        pltpu.make_async_copy(landed, landed, out_recv.at[g]).wait()
        lax.fori_loop(g * several, (g + 1) * several, convolve, carry)
        pltpu.make_async_copy(
            result.at[group(g), rows(me), :], conv_ref.at[group(g), :, columns(me)], home_recv.at[g]
        ).start()

        def one(step, inner):
            target = peer(step)
            pltpu.make_async_remote_copy(
                src_ref=result.at[group(g), rows(target), :],
                dst_ref=conv_ref.at[group(g), :, columns(me)],
                send_sem=home_send.at[g],
                recv_sem=home_recv.at[g],
                device_id=place(target),
                device_id_type=MESH,
            ).start()
            return inner

        return lax.fori_loop(1, count, one, carry)

    lax.fori_loop(0, groups, send_home, 0)

    def store(s):
        return pltpu.make_async_copy(kv.at[s, 0], gated_ref.at[s], store_sem.at[s])

    def apply_gate(s, carry):
        kv[s, 0] = (gate[s].astype(jnp.float32) * conv_ref[s].astype(jnp.float32)).astype(jnp.bfloat16)
        store(s).start()
        return carry

    def drain(g, carry):
        sent = received.at[group(g), pl.ds(0, (count - 1) * tokens), :]
        home = conv_ref.at[group(g)]
        pltpu.make_async_copy(sent, sent, out_send.at[g]).wait()
        pltpu.make_async_copy(sent, sent, home_send.at[g]).wait()
        pltpu.make_async_copy(home, home, home_recv.at[g]).wait()
        lax.fori_loop(g * several, (g + 1) * several, apply_gate, carry)
        return carry

    gate_load.wait()
    lax.fori_loop(0, groups, drain, 0)

    def finish(s, carry):
        store(s).wait()
        return carry

    lax.fori_loop(0, seqs, finish, 0)


def split_body(projections, impulse, skip_gain):
    ctx_size, ch_size = lax.axis_size("ctx"), lax.axis_size("ch")
    seqs, tokens, _, width = projections.shape
    span = impulse.shape[0]
    length = ctx_size * ch_size * tokens
    high, low = split_table(span)
    features = jnp.transpose(projections, (0, 2, 1, 3))
    anywhere = pl.BlockSpec(memory_space=pl.ANY)
    hbm = pl.BlockSpec(memory_space=pltpu.HBM)
    vmem = pl.BlockSpec(memory_space=pltpu.VMEM)
    bf16, f32 = jnp.bfloat16, jnp.float32
    return pl.pallas_call(
        functools.partial(mixer_kernel, ctx_size, ch_size),
        out_shape=jax.ShapeDtypeStruct((seqs, tokens, width), bf16),
        in_specs=[hbm, hbm, vmem, hbm, hbm],
        out_specs=anywhere,
        scratch_shapes=[
            pltpu.VMEM((2 * span, span), bf16),
            pltpu.VMEM((2 * span, span), bf16),
            pltpu.VMEM((seqs, 2, tokens, width), bf16),
            pltpu.VMEM((seqs, tokens, width), bf16),
            pltpu.VMEM((seqs, tokens, width), bf16),
            pltpu.VMEM((seqs, tokens, width), bf16),
            pltpu.VMEM((seqs, length, LANES), bf16),
            pltpu.VMEM((seqs, length, LANES), bf16),
            pltpu.VMEM((2, span, LANES), f32),
            pltpu.VMEM((6, span, LANES), f32),
            pltpu.VMEM((span, 2 * span), bf16),
            pltpu.VMEM((span, 2 * span), bf16),
            pltpu.VMEM((2 * span, 2 * LANES), bf16),
            pltpu.VMEM((2 * span, 2 * LANES), bf16),
            pltpu.SemaphoreType.DMA((seqs,)),
            pltpu.SemaphoreType.DMA,
            pltpu.SemaphoreType.DMA((seqs,)),
            pltpu.SemaphoreType.DMA((2,)),
            pltpu.SemaphoreType.DMA((3,)),
            pltpu.SemaphoreType.DMA((seqs,)),
            pltpu.SemaphoreType.DMA((seqs,)),
            pltpu.SemaphoreType.DMA((seqs,)),
            pltpu.SemaphoreType.DMA((seqs,)),
        ],
        compiler_params=pltpu.CompilerParams(
            collective_id=0, has_side_effects=True, vmem_limit_bytes=60 * 1024 * 1024
        ),
    )(features, impulse, skip_gain.reshape(2, LANES), jnp.asarray(high), jnp.asarray(low))


def body(projections, impulse, skip_gain):
    ctx_size = lax.axis_size("ctx")
    whole_tiles = projections.shape[1] % 16 == 0 and impulse.shape[0] % 256 == 0
    if ctx_size == 2 and impulse.shape[1] == 2 * LANES and whole_tiles:
        return split_body(projections, impulse, skip_gain)
    return general_body(projections, impulse, skip_gain)


def solution(mesh):
    return jax.shard_map(
        body,
        mesh=mesh,
        in_specs=(P(None, ("ctx", "ch"), None, None), P("ctx", "ch"), P("ch")),
        out_specs=P(None, ("ctx", "ch"), None),
        check_vma=False,
    )
```

```python
import functools
import math

import jax
import jax.numpy as jnp
from jax import lax
from jax.experimental import pallas as pl
from jax.experimental.pallas import tpu as pltpu
from jax.sharding import PartitionSpec as P
import ml_dtypes
import numpy as np

MESH = pl.DeviceIdType.MESH
LANES = 128


def passed_along(value, axis, steps):
    count = lax.axis_size(axis)
    leading, last = (max(0, -steps), min(count, count - steps))
    return lax.ppermute(value, axis, [(source, source + steps) for source in range(leading, last)])


def forward_table(length):
    frequency = lax.broadcasted_iota(jnp.int32, (length, length), 0)
    sample = lax.broadcasted_iota(jnp.int32, (length, length), 1)
    angles = (frequency * sample % (2 * length)).astype(jnp.float32) * (math.pi / length)
    nyquist = jnp.where(sample % 2 == 0, jnp.float32(1.0), jnp.float32(-1.0))
    packed_imag = jnp.where(frequency == 0, nyquist, -jnp.sin(angles))
    return jnp.stack([jnp.cos(angles), packed_imag], axis=0)


def inverse_table(length):
    sample = lax.broadcasted_iota(jnp.int32, (2 * length, length), 0)
    frequency = lax.broadcasted_iota(jnp.int32, (2 * length, length), 1)
    angles = (frequency * sample % (2 * length)).astype(jnp.float32) * (math.pi / length)
    weight = jnp.where(frequency == 0, jnp.float32(0.5), jnp.float32(1.0)) / length
    nyquist = jnp.where(sample % 2 == 0, jnp.float32(0.5), jnp.float32(-0.5)) / length
    imag_part = jnp.where(frequency == 0, nyquist, -weight * jnp.sin(angles))
    return jnp.stack([weight * jnp.cos(angles), imag_part], axis=1)


def spectral_product(left_side, right_side):
    left_real = left_side[..., 0, :, :]
    left_imag = left_side[..., 1, :, :]
    right_real = right_side[..., 0, :, :]
    right_imag = right_side[..., 1, :, :]
    first_bin = lax.broadcasted_iota(jnp.int32, (left_real.shape[-2], 1), 0) == 0
    real_part = jnp.where(
        first_bin, left_real * right_real, left_real * right_real - left_imag * right_imag
    )
    imag_part = jnp.where(
        first_bin, left_imag * right_imag, left_real * right_imag + left_imag * right_real
    )
    return jnp.stack([real_part, imag_part], axis=-3)


def general_body(projections, impulse, skip_gain):
    length = impulse.shape[0]
    blocks = lax.axis_size("ctx")
    position = lax.axis_index("ctx")
    forward = forward_table(length)
    forward_low = forward.astype(jnp.bfloat16)
    received = lax.all_to_all(projections, "ch", split_axis=3, concat_axis=1, tiled=True)
    gate_part = received[:, :, 0, :]
    mixed_input = (
        received[:, :, 1, :].astype(jnp.float32) * received[:, :, 2, :].astype(jnp.float32)
    ).astype(jnp.bfloat16)
    spectrum, mixed_input, gate_rows = (
        jnp.einsum(
            "pkn,snc->spkc", forward_low, mixed_input, preferred_element_type=jnp.float32
        ).astype(jnp.bfloat16),
        mixed_input,
        gate_part,
    )
    own_filter = jnp.einsum("pkn,nc->pkc", forward, impulse, precision=lax.Precision.HIGHEST)
    filters = lax.all_gather(own_filter[None], "ctx", axis=0, tiled=True)
    zero_carry = jnp.zeros(spectrum.shape, jnp.float32)
    pieces = lax.all_gather(spectrum[None], "ctx", axis=0, tiled=True)
    current = zero_carry
    previous = zero_carry
    for offset in range(pieces.shape[0]):
        source = pieces[offset].astype(jnp.float32)
        lag_index = position - offset
        chosen = lax.dynamic_index_in_dim(
            filters, jnp.clip(lag_index, 0, blocks - 1), 0, keepdims=False
        )
        weight = (lag_index >= 0).astype(jnp.float32)
        current = current + spectral_product(source, chosen) * weight
    current, previous = (current, previous)
    inverse = inverse_table(length)
    signal = jnp.einsum("npk,spkc->snc", inverse, current, precision=lax.Precision.HIGHEST)
    head_part = signal[:, :length]
    tail_part = passed_along(signal[:, length:], "ctx", 1)
    mixed_wide = lax.optimization_barrier(mixed_input).astype(jnp.float32)
    convolved = head_part + tail_part + skip_gain * mixed_wide
    gated = (gate_rows.astype(jnp.float32) * convolved).astype(jnp.bfloat16)
    return lax.all_to_all(gated, "ch", split_axis=1, concat_axis=2, tiled=True)


def split_table(length):
    frequency = np.arange(length)[:, None]
    sample = np.arange(length)[None, :]
    angles = (frequency * sample % (2 * length)) * (math.pi / length)
    nyquist = np.where(sample % 2 == 0, 1.0, -1.0)
    imag = np.where(frequency == 0, nyquist, -np.sin(angles))
    table = np.concatenate([np.cos(angles), imag], axis=0)
    high = table.astype(ml_dtypes.bfloat16)
    low = (table - high.astype(np.float64)).astype(ml_dtypes.bfloat16)
    return high, low


def dot(left, right):
    return jnp.dot(left, right, preferred_element_type=jnp.float32)


def mixer_kernel(
    ctx_size, ch_size,
    proj_ref, impulse_ref, skip_ref, high_hbm, low_hbm,
    conv_ref,
    high_ref, low_ref,    kv, mixed, received, result, lags, coef, back_high, back_low, sum_high, sum_low,
    load_sem, table_sems, lag_sems, out_send, out_recv, home_send, home_recv,
):
    seqs, _, tokens, _ = proj_ref.shape
    span = impulse_ref.shape[0]
    count = ctx_size * ch_size
    y, c = lax.axis_index("ctx"), lax.axis_index("ch")
    me = y * ch_size + c
    tile = 128
    several = 2 if seqs % 2 == 0 else 1
    groups = seqs // several
    tiles = span // tile

    def place(device):
        return device // ch_size, device % ch_size

    def columns(device):
        py, pc = place(device)
        return pl.ds(pl.multiple_of((pc * ctx_size + py) * LANES, LANES), LANES)

    def rows(device):
        return pl.ds(pl.multiple_of(device * tokens, tokens), tokens)

    def peer(step):
        return lax.rem(me + step, count)

    def group(g):
        return pl.ds(g * several, several)

    def load(s):
        return pltpu.make_async_copy(proj_ref.at[s, pl.ds(1, 2)], kv.at[s], load_sem.at[s])

    barrier = pltpu.get_barrier_semaphore()

    def greet(step, carry):
        pl.semaphore_signal(barrier, inc=1, device_id=place(peer(step)), device_id_type=MESH)
        return carry

    lax.fori_loop(1, count, greet, 0)

    for s in range(seqs):
        load(s).start()
    own_lag = pltpu.make_async_copy(
        impulse_ref.at[:, pl.ds(pl.multiple_of(y * LANES, LANES), LANES)], lags.at[y], lag_sems.at[0]
    )
    own_lag.start()
    tables = [
        pltpu.make_async_copy(source, target, table_sems.at[i])
        for i, (source, target) in enumerate(((high_hbm, high_ref), (low_hbm, low_ref)))
    ]
    for table in tables:
        table.start()

    def multiply(s, carry):
        load(s).wait()
        mixed[s] = (kv[s, 0].astype(jnp.float32) * kv[s, 1].astype(jnp.float32)).astype(jnp.bfloat16)
        return carry

    lax.fori_loop(0, seqs, multiply, 0)

    pl.semaphore_wait(barrier, count - 1)

    other = 1 - y
    lag_copy = pltpu.make_async_remote_copy(
        src_ref=impulse_ref.at[:, pl.ds(pl.multiple_of(other * LANES, LANES), LANES)],
        dst_ref=lags.at[y],
        send_sem=lag_sems.at[1],
        recv_sem=lag_sems.at[2],
        device_id=(other, c),
        device_id_type=MESH,
    )
    def send_out(g, carry):
        pltpu.make_async_copy(
            mixed.at[group(g), :, columns(me)], received.at[group(g), rows(me), :], out_recv.at[g]
        ).start()

        def one(step, inner):
            target = peer(step)
            pltpu.make_async_remote_copy(
                src_ref=mixed.at[group(g), :, columns(target)],
                dst_ref=received.at[group(g), rows(me), :],
                send_sem=out_send.at[g],
                recv_sem=out_recv.at[g],
                device_id=place(target),
                device_id_type=MESH,
            ).start()
            return inner

        return lax.fori_loop(1, count, one, carry)

    send_out(0, 0)
    lag_copy.start()
    lax.fori_loop(1, groups, send_out, 0)
    for table in tables:
        table.wait()

    row = lax.broadcasted_iota(jnp.int32, (span, span), 0)
    col = lax.broadcasted_iota(jnp.int32, (span, span), 1)
    alternating = jnp.where(row % 2 == 0, jnp.float32(1.0), jnp.float32(-1.0))
    imag = high_ref[span:, :].astype(jnp.float32)
    imag = jnp.where(row == 0, jnp.float32(0.0), imag)
    back_high[:, :span] = high_ref[:span, :]
    back_high[:, span:] = jnp.where(col == 0, alternating, imag).astype(jnp.bfloat16)
    back_low[:, :span] = low_ref[:span, :]
    back_low[:, span:] = low_ref[span:, :]

    own_lag.wait()
    lag_copy.wait()
    taps = jnp.concatenate([lags[0], lags[1]], axis=1)
    taps_high = taps.astype(jnp.bfloat16)
    taps_low = (taps - taps_high.astype(jnp.float32)).astype(jnp.bfloat16)
    for t in range(tiles):
        parts = []
        for p in range(2):
            at = pl.ds(p * span + t * tile, tile)
            parts.append(
                dot(high_ref[at, :], taps_high)
                + dot(high_ref[at, :], taps_low)
                + dot(low_ref[at, :], taps_high)
            )
        real, imag = parts
        bins = lax.broadcasted_iota(jnp.int32, (tile, LANES), 0) + t * tile
        first = bins == 0
        sign = jnp.where(bins % 2 == 0, jnp.float32(1.0), jnp.float32(-1.0))
        weight = jnp.where(first, jnp.float32(0.5 / span), jnp.float32(1.0 / span))
        re0, im0 = real[:, :LANES] * weight, imag[:, :LANES] * weight
        re1 = real[:, LANES:] * weight + sign * re0
        im1 = imag[:, LANES:] * weight + sign * im0
        at = pl.ds(t * tile, tile)
        for base, re, im in ((0, re0, im0), (3, re1, im1)):
            coef[base, at, :] = re
            coef[base + 1, at, :] = jnp.where(first, jnp.float32(0.0), im)
            coef[base + 2, at, :] = jnp.where(first, im, re)

    def convolve(s, carry):
        signal = jnp.concatenate([received[s, :span, :], received[s, span:, :]], axis=1)
        for t in range(tiles):
            at = pl.ds(t * tile, tile)
            re = dot(high_ref[at, :], signal).astype(jnp.bfloat16).astype(jnp.float32)
            im = dot(high_ref[pl.ds(span + t * tile, tile), :], signal)
            im = im.astype(jnp.bfloat16).astype(jnp.float32)
            re0, re1 = re[:, :LANES], re[:, LANES:]
            im0, im1 = im[:, :LANES], im[:, LANES:]
            a0, b0, c0 = coef[0, at, :], coef[1, at, :], coef[2, at, :]
            a1, b1, c1 = coef[3, at, :], coef[4, at, :], coef[5, at, :]
            sums = (
                (re0 * a0 - im0 * b0, im0 * c0 + re0 * b0),
                (
                    re0 * a1 - im0 * b1 + (re1 * a0 - im1 * b0),
                    im0 * c1 + re0 * b1 + (im1 * c0 + re1 * b0),
                ),
            )
            for p in range(2):
                total = jnp.concatenate([sums[0][p], sums[1][p]], axis=1)
                high = total.astype(jnp.bfloat16)
                into = pl.ds(p * span + t * tile, tile)
                sum_high[into, :] = high
                sum_low[into, :] = (total - high.astype(jnp.float32)).astype(jnp.bfloat16)
        gain = skip_ref[pl.ds(y, 1), :]
        for t in range(tiles):
            at = pl.ds(t * tile, tile)
            response = (
                dot(back_high[at, :], sum_high[...])
                + dot(back_high[at, :], sum_low[...])
                + dot(back_low[at, :], sum_high[...])
            )
            for j in range(2):
                into = pl.ds(j * span + t * tile, tile)
                direct = gain * received[s, into, :].astype(jnp.float32)
                result[s, into, :] = (
                    response[:, j * LANES : (j + 1) * LANES] + direct
                ).astype(jnp.bfloat16)
        return carry

    def send_home(g, carry):
        landed = received.at[group(g)]
        pltpu.make_async_copy(landed, landed, out_recv.at[g]).wait()
        lax.fori_loop(g * several, (g + 1) * several, convolve, carry)
        pltpu.make_async_copy(
            result.at[group(g), rows(me), :], conv_ref.at[group(g), :, columns(me)], home_recv.at[g]
        ).start()

        def one(step, inner):
            target = peer(step)
            pltpu.make_async_remote_copy(
                src_ref=result.at[group(g), rows(target), :],
                dst_ref=conv_ref.at[group(g), :, columns(me)],
                send_sem=home_send.at[g],
                recv_sem=home_recv.at[g],
                device_id=place(target),
                device_id_type=MESH,
            ).start()
            return inner

        return lax.fori_loop(1, count, one, carry)

    lax.fori_loop(0, groups, send_home, 0)

    def drain(g, carry):
        sent = received.at[group(g), pl.ds(0, (count - 1) * tokens), :]
        home = conv_ref.at[group(g)]
        pltpu.make_async_copy(sent, sent, out_send.at[g]).wait()
        pltpu.make_async_copy(sent, sent, home_send.at[g]).wait()
        pltpu.make_async_copy(home, home, home_recv.at[g]).wait()
        return carry

    lax.fori_loop(0, groups, drain, 0)


def split_body(projections, impulse, skip_gain):
    ctx_size, ch_size = lax.axis_size("ctx"), lax.axis_size("ch")
    seqs, tokens, _, width = projections.shape
    span = impulse.shape[0]
    length = ctx_size * ch_size * tokens
    high, low = split_table(span)
    features = jnp.transpose(projections, (0, 2, 1, 3))
    anywhere = pl.BlockSpec(memory_space=pl.ANY)
    hbm = pl.BlockSpec(memory_space=pltpu.HBM)
    vmem = pl.BlockSpec(memory_space=pltpu.VMEM)
    bf16, f32 = jnp.bfloat16, jnp.float32
    convolved = pl.pallas_call(
        functools.partial(mixer_kernel, ctx_size, ch_size),
        out_shape=jax.ShapeDtypeStruct((seqs, tokens, width), bf16),
        in_specs=[hbm, hbm, vmem, hbm, hbm],
        out_specs=anywhere,
        scratch_shapes=[
            pltpu.VMEM((2 * span, span), bf16),
            pltpu.VMEM((2 * span, span), bf16),
            pltpu.VMEM((seqs, 2, tokens, width), bf16),
            pltpu.VMEM((seqs, tokens, width), bf16),
            pltpu.VMEM((seqs, length, LANES), bf16),
            pltpu.VMEM((seqs, length, LANES), bf16),
            pltpu.VMEM((2, span, LANES), f32),
            pltpu.VMEM((6, span, LANES), f32),
            pltpu.VMEM((span, 2 * span), bf16),
            pltpu.VMEM((span, 2 * span), bf16),
            pltpu.VMEM((2 * span, 2 * LANES), bf16),
            pltpu.VMEM((2 * span, 2 * LANES), bf16),
            pltpu.SemaphoreType.DMA((seqs,)),
            pltpu.SemaphoreType.DMA((2,)),
            pltpu.SemaphoreType.DMA((3,)),
            pltpu.SemaphoreType.DMA((seqs,)),
            pltpu.SemaphoreType.DMA((seqs,)),
            pltpu.SemaphoreType.DMA((seqs,)),
            pltpu.SemaphoreType.DMA((seqs,)),
        ],
        compiler_params=pltpu.CompilerParams(
            collective_id=0, has_side_effects=True, vmem_limit_bytes=40 * 1024 * 1024
        ),
    )(*(pltpu.with_memory_space_constraint(x, pltpu.HBM) for x in (features, impulse, skip_gain.reshape(2, LANES), jnp.asarray(high), jnp.asarray(low))))
    gate = features[:, 0]
    return (gate.astype(f32) * convolved.astype(f32)).astype(bf16)


def body(projections, impulse, skip_gain):
    ctx_size = lax.axis_size("ctx")
    whole_tiles = projections.shape[1] % 16 == 0 and impulse.shape[0] % 256 == 0
    if ctx_size == 2 and impulse.shape[1] == 2 * LANES and whole_tiles:
        return split_body(projections, impulse, skip_gain)
    return general_body(projections, impulse, skip_gain)


def solution(mesh):
    return jax.shard_map(
        body,
        mesh=mesh,
        in_specs=(P(None, ("ctx", "ch"), None, None), P("ctx", "ch"), P("ch")),
        out_specs=P(None, ("ctx", "ch"), None),
        check_vma=False,
    )
```
